32 devices in a mesh: groups: 2 (over x), branch: 4 (over y, core), head: 4 (over z).
Axes of the slice: x: 2, y: 2, z: 4, core: 2. Of those that a mesh axis runs over, the one named last changes fastest.
Arguments:
- queries: bfloat16 [128, 8192], P(('groups', 'branch'), 'head'), parts along dimension 0, may hold values from -100 to 100, as said below
- root_keys: bfloat16 [32768, 1024], P(('groups', 'branch'), 'head'), parts along dimension 0, may hold values from -6 to 6
- root_values: bfloat16 [32768, 1024], P(('groups', 'branch'), 'head'), parts along dimension 0, may hold values from -6 to 6
- branch_keys: bfloat16 [8, 4096, 1024], P(('groups', 'branch'), None, 'head'), parts along dimension 0, may hold values from -6 to 6
- branch_values: bfloat16 [8, 4096, 1024], P(('groups', 'branch'), None, 'head'), parts along dimension 0, may hold values from -6 to 6
- branch_lengths: int32 [8], P(('groups', 'branch')), parts along dimension 0, may hold values from 512 to 4096, as said below
- row_branch: int32 [128], P('groups'), parts along dimension 0, may hold values from 0 to 3, as said below
Outputs:
- attended: bfloat16 [128, 8192], P(('groups', 'branch'), 'head'), parts along dimension 0
The draws below stay inside these ranges and needn't reach their ends.
There are 2 independent parts, one for each index of `groups`. The reference program is written for one: setup_inputs(seed, part) draws one part's arguments, and reference() takes and returns one part's arrays. A program takes and returns all parts, laid end to end along the dimension named above; each array names one. Nothing has to cross between parts.
Inputs may be any that keep to these rules, and one draw needn't show every extreme that they name: `queries`: query entries; rows may differ in scale. `row_branch`: no branch has more than 32 rows; some branch has exactly 32. `branch_lengths`: some branch has exactly 4096 live tokens.
All inputs are finite; a program needn't handle non-finite values.
Results may differ from the reference program's by a relative error of at most 0.006.
Values may be sent and summed in bfloat16 or wider, within the bound.
A program may use at most 128 MiB of HBM per device.

```python
import jax
import jax.numpy as jnp
from jax import lax

QHEADS = 64
KVHEADS = 8
HD = 128
BMAX = 4096
BRANCHES = 4
ROWS = 64
MOST = 32
ROOT = 16384


def draw_queries(key, part):
    first = jax.random.fold_in(jax.random.fold_in(key, 5), 0)
    base = 3.0 * jax.random.normal(first, (ROWS, QHEADS * HD), jnp.float32)
    return jnp.clip(base, -15.0, 15.0).astype(jnp.bfloat16)


def draw_row_branch(key, part):
    first, second, third = jax.random.split(jax.random.fold_in(key, 11), 3)
    heavy = jax.random.randint(first, (), 0, BRANCHES)
    slots = jnp.arange((BRANCHES - 1) * MOST, dtype=jnp.int32) // MOST
    slots = slots + (slots >= heavy).astype(jnp.int32)
    chosen = jax.random.permutation(second, slots)[:ROWS - MOST]
    assigned = jnp.concatenate([jnp.full((MOST,), heavy, jnp.int32), chosen])
    return jax.random.permutation(third, assigned).astype(jnp.int32)


def draw_branch_lengths(key, part):
    first, second = jax.random.split(jax.random.fold_in(key, 23))
    lengths = jax.random.randint(first, (BRANCHES,), BMAX // 8, BMAX + 1)
    longest = jax.random.randint(second, (), 0, BRANCHES)
    return jnp.where(jnp.arange(BRANCHES) == longest, BMAX, lengths).astype(jnp.int32)


def steps_of(key, dims, cuts, least, top_value):
    gain = 1.0
    for position, shards_of in cuts:
        draws = jax.random.uniform(jax.random.fold_in(jax.random.fold_in(key, 6), position), (shards_of,), jnp.float32, least / len(cuts), top_value / len(cuts))
        gain = gain * jnp.repeat(jnp.exp(draws), dims[position] // shards_of).reshape((-1,) + (1,) * (len(dims) - 1 - position))
    return gain


def noise(stream_key, dims, spread, most, cuts=(), kind=jnp.bfloat16):
    level = steps_of(stream_key, dims, cuts, -0.22, 0.18) if cuts else 1.0
    values = jax.random.normal(stream_key, dims, jnp.float32) * spread * level
    return jnp.minimum(jnp.maximum(values, -most), most).astype(kind)


def setup_inputs(seed: int = 0, part: int = 0) -> dict:
    streams_of = jax.random.split(jax.random.key(seed), 8)
    part_keys = jax.random.split(jax.random.fold_in(streams_of[7], part), 8)
    queries = draw_queries(jax.random.fold_in(jax.random.fold_in(streams_of[7], part), 71), part)
    root_keys = noise(part_keys[1], (ROOT, KVHEADS * HD), 1.0, 6.0, ((0, 4), (1, 4)))
    root_values = noise(part_keys[2], (ROOT, KVHEADS * HD), 1.0, 6.0, ((0, 4), (1, 4)))
    branch_keys = noise(part_keys[3], (BRANCHES, BMAX, KVHEADS * HD), 1.0, 6.0, ((0, 4), (2, 4)))
    branch_values = noise(part_keys[4], (BRANCHES, BMAX, KVHEADS * HD), 1.0, 6.0, ((0, 4), (2, 4)))
    branch_lengths = draw_branch_lengths(jax.random.fold_in(jax.random.fold_in(streams_of[7], part), 71), part)
    row_branch = draw_row_branch(jax.random.fold_in(jax.random.fold_in(streams_of[7], part), 71), part)
    return {"queries": queries, "root_keys": root_keys, "root_values": root_values, "branch_keys": branch_keys, "branch_values": branch_values, "branch_lengths": branch_lengths, "row_branch": row_branch}


NEG = -1.0e30


def empty_part(count):
    return (jnp.full((count, QHEADS), NEG, jnp.float32), jnp.zeros((count, QHEADS), jnp.float32), jnp.zeros((count, QHEADS, HD), jnp.float32))


def combine(first, second):
    peak = jnp.maximum(first[0], second[0])
    scale_a = jnp.exp(first[0] - peak)
    scale_b = jnp.exp(second[0] - peak)
    return (peak, first[1] * scale_a + second[1] * scale_b, first[2] * scale_a[..., None] + second[2] * scale_b[..., None])


def partial_block(query, keys, values, valid):
    count = query.shape[0]
    scores = jnp.einsum("rgph,bgh->rgpb", query.astype(jnp.float32), keys.astype(jnp.float32)) * (HD ** -0.5)
    scores = jnp.where(valid, scores, NEG)
    peak = jnp.max(scores, axis=-1)
    weights = jnp.where(valid, jnp.exp(scores - peak[..., None]), 0.0)
    total = jnp.sum(weights, axis=-1)
    rounded = lax.optimization_barrier(weights.astype(jnp.bfloat16)).astype(jnp.float32)
    mixed = jnp.einsum("rgpb,bgh->rgph", rounded, values.astype(jnp.float32))
    return (peak.reshape(count, QHEADS), total.reshape(count, QHEADS), mixed.reshape(count, QHEADS, HD))


def reference(queries, root_keys, root_values, branch_keys, branch_values, branch_lengths, row_branch):
    per_group = QHEADS // KVHEADS
    query = queries.reshape(ROWS, KVHEADS, per_group, HD)
    block = min(512, ROOT)
    root_k = root_keys.reshape(ROOT // block, block, KVHEADS, HD)
    root_v = root_values.reshape(ROOT // block, block, KVHEADS, HD)

    def root_step(carry, pair):
        return combine(carry, partial_block(query, pair[0], pair[1], jnp.ones((block,), dtype=bool))), None

    root_part, _ = lax.scan(root_step, empty_part(ROWS), (root_k, root_v))
    inner = min(512, BMAX)
    slot_ids = jnp.arange(MOST, dtype=jnp.int32)
    positions = jnp.arange(BMAX, dtype=jnp.int32).reshape(BMAX // inner, inner)

    def branch_step(carry, index):
        member = row_branch == index
        ranking = jnp.cumsum(member.astype(jnp.int32)) - 1
        picker = member[None, :] & (ranking[None, :] == slot_ids[:, None])
        pick = picker.astype(jnp.float32)
        chosen = jnp.dot(pick, queries.astype(jnp.float32), precision=lax.Precision.HIGHEST).reshape(MOST, KVHEADS, per_group, HD)
        keys = lax.dynamic_index_in_dim(branch_keys, index, 0, keepdims=False).reshape(BMAX // inner, inner, KVHEADS, HD)
        values = lax.dynamic_index_in_dim(branch_values, index, 0, keepdims=False).reshape(BMAX // inner, inner, KVHEADS, HD)
        length = lax.dynamic_index_in_dim(branch_lengths, index, 0, keepdims=False)

        def key_step(state, triple):
            return combine(state, partial_block(chosen, triple[0], triple[1], triple[2] < length)), None

        part, _ = lax.scan(key_step, empty_part(MOST), (keys, values, positions))
        spread_peak = jnp.max(jnp.where(picker[:, :, None], part[0][:, None, :], NEG), axis=0)
        spread_total = jnp.einsum("sr,sk->rk", pick, part[1], precision=lax.Precision.HIGHEST)
        spread_mixed = jnp.einsum("sr,sk->rk", pick, part[2].reshape(MOST, QHEADS * HD), precision=lax.Precision.HIGHEST)
        return combine(carry, (spread_peak, spread_total, spread_mixed.reshape(ROWS, QHEADS, HD))), None

    branch_part, _ = lax.scan(branch_step, empty_part(ROWS), jnp.arange(BRANCHES, dtype=jnp.int32))
    peak, total, mixed = combine(root_part, branch_part)
    return (mixed / total[..., None]).reshape(ROWS, QHEADS * HD).astype(jnp.bfloat16)
```

```python
import functools
import math

import jax
import jax.numpy as jnp
from jax import lax
from jax.experimental import pallas as pl
from jax.experimental.pallas import tpu as pltpu
from jax.sharding import PartitionSpec as P

HD = 128
PER = 8
NEG = -1e30
MESH = pl.DeviceIdType.MESH
BF = jnp.bfloat16
F32 = jnp.float32


def split(value, parts):
    pieces = []
    for _ in range(parts):
        piece = value.astype(BF)
        pieces.append(piece)
        value = value - piece.astype(F32)
    return pieces


def kernel(
    n, rows, tokens, groups, tb,
    q_ref, rb_ref, len_ref, rk_ref, rv_ref, bk_ref, bv_ref, out_ref,
    qall, kbuf, vbuf, qbr, sbuf, mbuf, acc, rnum, rm, spread_e,
    send_o, send_l, recv_o, recv_l,
    kv_sem, q_own, q_send, q_recv, o_send, o_recv, l_send, l_recv,
):
    me = lax.axis_index("branch")
    slots = 2 * rows
    m_rows = slots * PER
    chunks = n // 2
    all_rows = n * rows
    part = rows * PER
    blocks = tokens // tb
    factor = math.log2(math.e) / math.sqrt(HD)

    copies = [
        pltpu.make_async_copy(src, dst, kv_sem.at[i])
        for i, (src, dst) in enumerate((
            (rk_ref, kbuf.at[0]), (rv_ref, vbuf.at[0]),
            (bk_ref.at[0], kbuf.at[1]), (bv_ref.at[0], vbuf.at[1]),
        ))
    ]
    own = pltpu.make_async_copy(q_ref, qall.at[me], q_own)
    own.start()
    for copy in copies:
        copy.start()

    barrier = pltpu.get_barrier_semaphore()
    for off in range(1, n):
        peer = me ^ off
        pl.semaphore_signal(barrier, inc=1, device_id={"branch": peer}, device_id_type=MESH)
    pl.semaphore_wait(barrier, n - 1)

    q_copies = []
    for off in range(1, n):
        peer = me ^ off
        copy = pltpu.make_async_remote_copy(
            src_ref=q_ref, dst_ref=qall.at[me], send_sem=q_send.at[off],
            recv_sem=q_recv.at[off], device_id={"branch": peer}, device_id_type=MESH,
        )
        copy.start()
        q_copies.append(copy)

    rb = rb_ref[...]
    mem_row = jnp.where(rb == me, 1.0, 0.0).astype(F32)
    r_sub = lax.broadcasted_iota(jnp.int32, (all_rows, all_rows), 0)
    r_lane = lax.broadcasted_iota(jnp.int32, (all_rows, all_rows), 1)
    mem_b = jnp.broadcast_to(mem_row, (all_rows, all_rows))
    mem_col = jnp.sum(jnp.where(r_sub == r_lane, mem_b, 0.0), axis=1, keepdims=True)
    rank_col = jnp.sum(jnp.where(r_lane < r_sub, mem_b, 0.0), axis=1, keepdims=True)
    mem_cb = jnp.broadcast_to(mem_col, (all_rows, all_rows))
    rank_row = jnp.sum(jnp.where(r_sub < r_lane, mem_cb, 0.0), axis=0, keepdims=True)
    slot_sub = lax.broadcasted_iota(jnp.int32, (slots, all_rows), 0).astype(F32)
    picker = jnp.where(
        (jnp.broadcast_to(rank_row, (slots, all_rows)) == slot_sub)
        & (jnp.broadcast_to(mem_row, (slots, all_rows)) > 0.5), 1.0, 0.0,
    ).astype(BF)
    slot_lane = lax.broadcasted_iota(jnp.int32, (all_rows, slots), 1).astype(F32)
    e_full = jnp.where(
        (jnp.broadcast_to(rank_col, (all_rows, slots)) == slot_lane)
        & (jnp.broadcast_to(mem_col, (all_rows, slots)) > 0.5), 1.0, 0.0,
    ).astype(BF)
    spread_e[...] = e_full
    length = len_ref[0]

    def stack(q, g):
        return jnp.concatenate(
            [q[:, (g * PER + p) * HD:(g * PER + p + 1) * HD] for p in range(PER)], axis=0
        )

    def chunk_of(k):
        return lax.rem(me // 2 + k, chunks)

    tasks = []
    for g in range(groups):
        tasks.append((0, g, 0))
    for g in range(groups):
        for k in range(1, chunks):
            tasks.append((0, g, k))
        tasks.append((1, g, 0))

    waited = set()

    def need(index):
        if index not in waited:
            waited.add(index)
            copies[index].wait()

    def need_q(off):
        key = ("q", off)
        if key not in waited:
            waited.add(key)
            if off == 0:
                own.wait()
            else:
                q_copies[off - 1].wait_recv()

    def stage(first, second, slot):
        if first is not None:
            src, g, k = first
            need(2 * src)
            if src == 0:
                need_q(2 * k)
                need_q(2 * k + 1)
                base = (me // 2) ^ k
                q_here = qall[pl.ds(base * 2, 2)].reshape(slots, groups * PER * HD)
                query = stack(q_here, g)
            else:
                for off in range(n):
                    need_q(off)
                if g == 0:
                    whole = qall[...].reshape(all_rows, groups * PER * HD)
                    qbr[...] = jnp.dot(picker, whole, preferred_element_type=F32).astype(BF)
                query = stack(qbr[...], g)
            mbuf[slot] = jnp.full((m_rows, HD), NEG, F32)
        if second is not None:
            src2, g2, k2 = second
            need(2 * src2 + 1)
            other = 1 - slot
            peak = jnp.max(mbuf[other], axis=1, keepdims=True) * factor
            mbuf[other] = jnp.broadcast_to(peak, (m_rows, HD))
            acc[...] = jnp.zeros_like(acc)

        def body(j, carry):
            start = pl.multiple_of(j * tb, tb)
            if first is not None:
                keys = kbuf[src, pl.ds(start, tb), g * HD:(g + 1) * HD]
                score = lax.dot_general(
                    query, keys, (((1,), (1,)), ((), ())), preferred_element_type=F32
                )
                if src == 1:
                    place = start + lax.broadcasted_iota(jnp.int32, (m_rows, tb), 1)
                    score = jnp.where(place < length, score, NEG)
                top = score[:, :HD]
                for i in range(1, tb // HD):
                    top = jnp.maximum(top, score[:, i * HD:(i + 1) * HD])
                sbuf[slot, j] = score
                mbuf[slot] = jnp.maximum(mbuf[slot], top)
            if second is not None:
                top2 = mbuf[other]
                peaks = jnp.concatenate([top2] * (tb // HD), axis=1)
                weights = jnp.exp2(sbuf[other, j] * factor - peaks).astype(BF)
                values = vbuf[src2, pl.ds(start, tb), g2 * HD:(g2 + 1) * HD]
                wide = jnp.concatenate([values, jnp.ones((tb, HD), BF)], axis=1)
                acc[...] += jnp.dot(weights, wide, preferred_element_type=F32)
            return carry

        lax.fori_loop(0, blocks, body, 0)

        if second is not None and src2 == 0:
            rnum[g2, k2] = acc[...]
            rm[g2, k2] = mbuf[other]

    eye = (
        lax.broadcasted_iota(jnp.int32, (part, part), 0)
        == lax.broadcasted_iota(jnp.int32, (part, part), 1)
    )
    sent = []

    def finish(g, other):
        numer = acc[:, :HD]
        total = acc[:, HD:]
        top = mbuf[other]
        rights = []
        for p in range(PER):
            lo, hi = p * slots, (p + 1) * slots
            a = jnp.concatenate(split(numer[lo:hi], 2) + [jnp.zeros((slots, HD), BF)], axis=0)
            b = jnp.concatenate(split(total[lo:hi], 2) + [jnp.zeros((slots, HD), BF)], axis=0)
            c = jnp.concatenate(split(top[lo:hi], 3), axis=0)
            rights.append(jnp.concatenate([a, b, c], axis=1))
        for k in range(chunks):
            base = (me // 2) ^ k
            e = spread_e[pl.ds(pl.multiple_of(base * slots, slots), slots), :]
            e3 = jnp.concatenate([e, e, e], axis=1)
            has = jnp.sum(e.astype(F32), axis=1, keepdims=True) > 0.5
            has = jnp.broadcast_to(has, (slots, HD))
            whole_o, whole_l = [], []
            for p in range(PER):
                lo, hi = p * slots, (p + 1) * slots
                back = jnp.dot(e3, rights[p], preferred_element_type=F32)
                r_num = rnum[g, k, lo:hi, :HD]
                r_tot = rnum[g, k, lo:hi, HD:]
                r_top = rm[g, k, lo:hi]
                b_top = jnp.where(has, back[:, 2 * HD:], NEG)
                peak = jnp.maximum(r_top, b_top)
                x = jnp.exp2(r_top - peak)
                y = jnp.exp2(b_top - peak)
                num = r_num * x + back[:, :HD] * y
                tot = r_tot * x + back[:, HD:2 * HD] * y
                whole_o.append((num / tot).astype(BF))
                whole_l.append(peak + jnp.log2(tot))
            for half in range(2):
                off_slot = 2 * k + half
                lo, hi = half * rows, (half + 1) * rows
                send_o[g, off_slot] = jnp.concatenate([o[lo:hi] for o in whole_o], axis=0)
                lse = jnp.concatenate([v[lo:hi] for v in whole_l], axis=0)
                line = jnp.sum(jnp.where(eye, lse, 0.0), axis=0, keepdims=True)
                send_l[g, off_slot] = jnp.broadcast_to(line, (8, part))
        for off in range(1, n):
            k = off // 2
            peer = me ^ off
            index = 2 * k + lax.rem(peer, 2)
            pair = []
            for src, dst, s_sem, r_sem in (
                (send_o, recv_o, o_send, o_recv), (send_l, recv_l, l_send, l_recv),
            ):
                copy = pltpu.make_async_remote_copy(
                    src_ref=src.at[g, index], dst_ref=dst.at[g, off],
                    send_sem=s_sem.at[g, off], recv_sem=r_sem.at[g, off],
                    device_id={"branch": peer}, device_id_type=MESH,
                )
                copy.start()
                pair.append(copy)
            sent.append((g, off, pair))

    def collect(g):
        mine = lax.rem(me, 2)
        lines = [send_l[g, mine][:1]]
        outs = [send_o[g, mine]]
        for gg, off, pair in sent:
            if gg == g:
                for copy in pair:
                    copy.wait_recv()
                lines.append(recv_l[g, off][:1])
                outs.append(recv_o[g, off])
        peak = functools.reduce(jnp.maximum, lines)
        scales = [jnp.exp2(line - peak) for line in lines]
        inverse = 1.0 / functools.reduce(jnp.add, scales)
        result = jnp.zeros((part, HD), F32)
        for scale, o in zip(scales, outs):
            diag = jnp.where(eye, jnp.broadcast_to(scale * inverse, (part, part)), 0.0)
            left = jnp.concatenate(split(diag, 2), axis=1)
            result += jnp.dot(left, jnp.concatenate([o, o], axis=0), preferred_element_type=F32)
        result = result.astype(BF)
        for p in range(PER):
            out_ref[:, (g * PER + p) * HD:(g * PER + p + 1) * HD] = result[p * rows:(p + 1) * rows]

    previous = None
    for t, task in enumerate(tasks + [None]):
        stage(task, previous, t % 2)
        if previous is not None and previous[0] == 1:
            finish(previous[1], 1 - t % 2)
        previous = task
    for g in range(groups):
        collect(g)
    for copy in q_copies:
        copy.wait_send()
    for _, _, pair in sent:
        for copy in pair:
            copy.wait_send()


def on_device(
    queries, root_keys, root_values, branch_keys, branch_values, branch_lengths, row_branch
):
    rows = queries.shape[0]
    all_rows = row_branch.shape[0]
    n = all_rows // rows
    tokens, width = root_keys.shape
    groups = width // HD
    chunks = n // 2
    slots = 2 * rows
    m_rows = slots * PER
    part = rows * PER
    tb = min(1024, tokens)
    vmem = pl.BlockSpec(memory_space=pltpu.VMEM)
    smem = pl.BlockSpec(memory_space=pltpu.SMEM)
    hbm = pl.BlockSpec(memory_space=pl.ANY)
    dma = pltpu.SemaphoreType.DMA
    return pl.pallas_call(
        functools.partial(kernel, n, rows, tokens, groups, tb),
        out_shape=jax.ShapeDtypeStruct(queries.shape, BF),
        in_specs=[vmem, vmem, smem, hbm, hbm, hbm, hbm],
        out_specs=vmem,
        scratch_shapes=[
            pltpu.VMEM((n, rows, groups * PER * HD), BF),
            pltpu.VMEM((2, tokens, width), BF),
            pltpu.VMEM((2, tokens, width), BF),
            pltpu.VMEM((slots, groups * PER * HD), BF),
            pltpu.VMEM((2, tokens // tb, m_rows, tb), F32),
            pltpu.VMEM((2, m_rows, HD), F32),
            pltpu.VMEM((m_rows, 2 * HD), F32),
            pltpu.VMEM((groups, chunks, m_rows, 2 * HD), F32),
            pltpu.VMEM((groups, chunks, m_rows, HD), F32),
            pltpu.VMEM((all_rows, slots), BF),
            pltpu.VMEM((groups, n, part, HD), BF),
            pltpu.VMEM((groups, n, 8, part), F32),
            pltpu.VMEM((groups, n, part, HD), BF),
            pltpu.VMEM((groups, n, 8, part), F32),
            dma((4,)), dma, dma((n,)), dma((n,)),
            dma((groups, n)), dma((groups, n)), dma((groups, n)), dma((groups, n)),
        ],
        compiler_params=pltpu.CompilerParams(
            collective_id=0, has_side_effects=True, vmem_limit_bytes=60 * 1024 * 1024
        ),
        name="cascade",
    )(queries, row_branch.reshape(1, all_rows), branch_lengths, root_keys, root_values, branch_keys, branch_values)


def solution(mesh):
    placed = (
        P(("groups", "branch"), "head"),
        P(("groups", "branch"), "head"),
        P(("groups", "branch"), "head"),
        P(("groups", "branch"), None, "head"),
        P(("groups", "branch"), None, "head"),
        P(("groups", "branch")),
        P("groups"),
    )
    return jax.shard_map(
        on_device,
        mesh=mesh,
        in_specs=placed,
        out_specs=P(("groups", "branch"), "head"),
        check_vma=False,
    )
```

```python
import functools
import math

import jax
import jax.numpy as jnp
from jax import lax
from jax.experimental import pallas as pl
from jax.experimental.pallas import tpu as pltpu
from jax.sharding import PartitionSpec as P

HD = 128
PER = 8
NEG = -1e30
MESH = pl.DeviceIdType.MESH
BF = jnp.bfloat16
F32 = jnp.float32


def split(value, parts):
    pieces = []
    for _ in range(parts):
        piece = value.astype(BF)
        pieces.append(piece)
        value = value - piece.astype(F32)
    return pieces


def kernel(
    n, rows, tokens, groups, tb,
    q_ref, rb_ref, len_ref, rk_ref, rv_ref, bk_ref, bv_ref, out_ref,
    qall, kbuf, vbuf, sbuf, mbuf, acc, rnum, rm, right, spread_e,
    send_o, send_l, recv_o, recv_l,
    kv_sem, q_own, q_send, q_recv, o_send, o_recv, l_send, l_recv,
):
    me = lax.axis_index("branch")
    slots = 2 * rows
    m_rows = slots * PER
    chunks = n // 2
    all_rows = n * rows
    part = rows * PER
    blocks = tokens // tb
    factor = math.log2(math.e) / math.sqrt(HD)

    copies = [
        pltpu.make_async_copy(src, dst, kv_sem.at[i])
        for i, (src, dst) in enumerate((
            (rk_ref, kbuf.at[0]), (rv_ref, vbuf.at[0]),
            (bk_ref.at[0], kbuf.at[1]), (bv_ref.at[0], vbuf.at[1]),
        ))
    ]
    own = pltpu.make_async_copy(q_ref, qall.at[me], q_own)
    own.start()
    copies[2].start()

    barrier = pltpu.get_barrier_semaphore()
    for off in range(1, n):
        peer = me ^ off
        pl.semaphore_signal(barrier, inc=1, device_id={"branch": peer}, device_id_type=MESH)
    pl.semaphore_wait(barrier, n - 1)

    q_copies = {}
    for g in range(groups):
        for off in range(1, n):
            peer = me ^ off
            cols = pl.ds(g * PER * HD, PER * HD)
            copy = pltpu.make_async_remote_copy(
                src_ref=q_ref.at[:, cols], dst_ref=qall.at[me, :, cols],
                send_sem=q_send.at[g, off], recv_sem=q_recv.at[g, off],
                device_id={"branch": peer}, device_id_type=MESH,
            )
            copy.start()
            q_copies[g, off] = copy
    copies[3].start()

    rb = rb_ref[...]
    mem_row = jnp.where(rb == me, 1.0, 0.0).astype(F32)
    r_sub = lax.broadcasted_iota(jnp.int32, (all_rows, all_rows), 0)
    r_lane = lax.broadcasted_iota(jnp.int32, (all_rows, all_rows), 1)
    mem_b = jnp.broadcast_to(mem_row, (all_rows, all_rows))
    mem_col = jnp.sum(jnp.where(r_sub == r_lane, mem_b, 0.0), axis=1, keepdims=True)
    rank_col = jnp.sum(jnp.where(r_lane < r_sub, mem_b, 0.0), axis=1, keepdims=True)
    mem_cb = jnp.broadcast_to(mem_col, (all_rows, all_rows))
    rank_row = jnp.sum(jnp.where(r_sub < r_lane, mem_cb, 0.0), axis=0, keepdims=True)
    slot_sub = lax.broadcasted_iota(jnp.int32, (slots, all_rows), 0).astype(F32)
    picker = jnp.where(
        (jnp.broadcast_to(rank_row, (slots, all_rows)) == slot_sub)
        & (jnp.broadcast_to(mem_row, (slots, all_rows)) > 0.5), 1.0, 0.0,
    ).astype(BF)
    slot_lane = lax.broadcasted_iota(jnp.int32, (all_rows, slots), 1).astype(F32)
    e_full = jnp.where(
        (jnp.broadcast_to(rank_col, (all_rows, slots)) == slot_lane)
        & (jnp.broadcast_to(mem_col, (all_rows, slots)) > 0.5), 1.0, 0.0,
    ).astype(BF)
    spread_e[...] = e_full
    length = len_ref[0]

    def stack(q):
        return jnp.concatenate([q[:, p * HD:(p + 1) * HD] for p in range(PER)], axis=0)

    tasks = []
    for g in range(groups):
        tasks += [(1, g, 0)] + [(0, g, k) for k in range(1, chunks)]
    tasks += [(0, g, 0) for g in range(groups)]

    waited = set()
    started = {2, 3}

    def need(index):
        if index not in waited:
            waited.add(index)
            copies[index].wait()

    def launch(index):
        if index not in started:
            started.add(index)
            copies[index].start()

    def need_q(g, off):
        key = ("q", g, off)
        if key not in waited:
            waited.add(key)
            if off > 0:
                q_copies[g, off].wait_recv()
            elif ("own",) not in waited:
                waited.add(("own",))
                own.wait()

    def stage(first, second, slot):
        if first is not None:
            src, g, k = first
            cols = slice(g * PER * HD, (g + 1) * PER * HD)
            launch(2 * src)
            need(2 * src)
            launch(2 * src + 1)
            launch(0)
            if second is not None:
                launch(1)
            if src == 0:
                need_q(g, 2 * k)
                need_q(g, 2 * k + 1)
                base = (me // 2) ^ k
                query = stack(qall[pl.ds(base * 2, 2), :, cols].reshape(slots, PER * HD))
            else:
                for off in range(n):
                    need_q(g, off)
                whole = qall[:, :, cols].reshape(all_rows, PER * HD)
                query = stack(jnp.dot(picker, whole, preferred_element_type=F32).astype(BF))
            mbuf[slot] = jnp.full((m_rows, HD), NEG, F32)
        if second is not None:
            src2, g2, k2 = second
            need(2 * src2 + 1)
            other = 1 - slot
            peak = jnp.max(mbuf[other], axis=1, keepdims=True) * factor
            mbuf[other] = jnp.broadcast_to(peak, (m_rows, HD))
            acc[...] = jnp.zeros_like(acc)

        def body(j, carry):
            start = pl.multiple_of(j * tb, tb)
            if first is not None:
                keys = kbuf[src, pl.ds(start, tb), g * HD:(g + 1) * HD]
                score = lax.dot_general(
                    query, keys, (((1,), (1,)), ((), ())), preferred_element_type=F32
                )
                if src == 1:
                    place = start + lax.broadcasted_iota(jnp.int32, (m_rows, tb), 1)
                    score = jnp.where(place < length, score, NEG)
                top = score[:, :HD]
                for i in range(1, tb // HD):
                    top = jnp.maximum(top, score[:, i * HD:(i + 1) * HD])
                sbuf[slot, j] = score
                mbuf[slot] = jnp.maximum(mbuf[slot], top)
            if second is not None:
                top2 = mbuf[other]
                peaks = jnp.concatenate([top2] * (tb // HD), axis=1)
                weights = jnp.exp2(sbuf[other, j] * factor - peaks).astype(BF)
                values = vbuf[src2, pl.ds(start, tb), g2 * HD:(g2 + 1) * HD]
                wide = jnp.concatenate([values, jnp.ones((tb, HD), BF)], axis=1)
                acc[...] += jnp.dot(weights, wide, preferred_element_type=F32)
            return carry

        lax.fori_loop(0, blocks, body, 0)

        if second is not None and src2 == 0:
            rnum[g2, k2] = acc[...]
            rm[g2, k2] = mbuf[other]
        elif second is not None:
            numer, total, top = acc[:, :HD], acc[:, HD:], mbuf[other]
            for p in range(PER):
                lo, hi = p * slots, (p + 1) * slots
                gap = [jnp.zeros((slots, HD), BF)]
                pieces = (split(numer[lo:hi], 2) + gap, split(total[lo:hi], 2) + gap, split(top[lo:hi], 3))
                right[g2, p] = jnp.concatenate(
                    [jnp.concatenate(piece, axis=0) for piece in pieces], axis=1
                )

    eye = (
        lax.broadcasted_iota(jnp.int32, (part, part), 0)
        == lax.broadcasted_iota(jnp.int32, (part, part), 1)
    )
    sent = []

    def finish(g, k):
        base = (me // 2) ^ k
        e = spread_e[pl.ds(pl.multiple_of(base * slots, slots), slots), :]
        e3 = jnp.concatenate([e, e, e], axis=1)
        has = jnp.sum(e.astype(F32), axis=1, keepdims=True) > 0.5
        has = jnp.broadcast_to(has, (slots, HD))
        whole_o, whole_l = [], []
        for p in range(PER):
            lo, hi = p * slots, (p + 1) * slots
            back = jnp.dot(e3, right[g, p], preferred_element_type=F32)
            r_num = rnum[g, k, lo:hi, :HD]
            r_tot = rnum[g, k, lo:hi, HD:]
            r_top = rm[g, k, lo:hi]
            b_top = jnp.where(has, back[:, 2 * HD:], NEG)
            peak = jnp.maximum(r_top, b_top)
            x = jnp.exp2(r_top - peak)
            y = jnp.exp2(b_top - peak)
            num = r_num * x + back[:, :HD] * y
            tot = r_tot * x + back[:, HD:2 * HD] * y
            whole_o.append((num / tot).astype(BF))
            whole_l.append(peak + jnp.log2(tot))
        for half in range(2):
            off_slot = 2 * k + half
            lo, hi = half * rows, (half + 1) * rows
            send_o[g, off_slot] = jnp.concatenate([o[lo:hi] for o in whole_o], axis=0)
            lse = jnp.concatenate([v[lo:hi] for v in whole_l], axis=0)
            line = jnp.sum(jnp.where(eye, lse, 0.0), axis=0, keepdims=True)
            send_l[g, off_slot] = jnp.broadcast_to(line, (8, part))
        for off in range(max(1, 2 * k), 2 * k + 2):
            peer = me ^ off
            index = 2 * k + lax.rem(peer, 2)
            pair = []
            for src, dst, s_sem, r_sem in (
                (send_o, recv_o, o_send, o_recv), (send_l, recv_l, l_send, l_recv),
            ):
                copy = pltpu.make_async_remote_copy(
                    src_ref=src.at[g, index], dst_ref=dst.at[g, off],
                    send_sem=s_sem.at[g, off], recv_sem=r_sem.at[g, off],
                    device_id={"branch": peer}, device_id_type=MESH,
                )
                copy.start()
                pair.append(copy)
            sent.append((g, off, pair))

    def collect(g):
        mine = lax.rem(me, 2)
        lines = [send_l[g, mine][:1]]
        outs = [send_o[g, mine]]
        for gg, off, pair in sent:
            if gg == g:
                for copy in pair:
                    copy.wait_recv()
                lines.append(recv_l[g, off][:1])
                outs.append(recv_o[g, off])
        peak = functools.reduce(jnp.maximum, lines)
        scales = [jnp.exp2(line - peak) for line in lines]
        inverse = 1.0 / functools.reduce(jnp.add, scales)
        result = jnp.zeros((part, HD), F32)
        for scale, o in zip(scales, outs):
            diag = jnp.where(eye, jnp.broadcast_to(scale * inverse, (part, part)), 0.0)
            left = jnp.concatenate(split(diag, 2), axis=1)
            result += jnp.dot(left, jnp.concatenate([o, o], axis=0), preferred_element_type=F32)
        result = result.astype(BF)
        for p in range(PER):
            out_ref[:, (g * PER + p) * HD:(g * PER + p + 1) * HD] = result[p * rows:(p + 1) * rows]

    previous = None
    done, finished = set(), set()
    for t, task in enumerate(tasks + [None]):
        stage(task, previous, t % 2)
        if previous is not None:
            done.add(previous)
            for g in range(groups):
                for k in reversed(range(chunks)):
                    if (1, g, 0) in done and (0, g, k) in done and (g, k) not in finished:
                        finished.add((g, k))
                        finish(g, k)
        previous = task
    for g in range(groups):
        collect(g)
    for copy in q_copies.values():
        copy.wait_send()
    for _, _, pair in sent:
        for copy in pair:
            copy.wait_send()


def on_device(
    queries, root_keys, root_values, branch_keys, branch_values, branch_lengths, row_branch
):
    rows = queries.shape[0]
    all_rows = row_branch.shape[0]
    n = all_rows // rows
    tokens, width = root_keys.shape
    groups = width // HD
    chunks = n // 2
    slots = 2 * rows
    m_rows = slots * PER
    part = rows * PER
    tb = min(2048, tokens)
    vmem = pl.BlockSpec(memory_space=pltpu.VMEM)
    smem = pl.BlockSpec(memory_space=pltpu.SMEM)
    hbm = pl.BlockSpec(memory_space=pl.ANY)
    dma = pltpu.SemaphoreType.DMA
    return pl.pallas_call(
        functools.partial(kernel, n, rows, tokens, groups, tb),
        out_shape=jax.ShapeDtypeStruct(queries.shape, BF),
        in_specs=[vmem, vmem, smem, hbm, hbm, hbm, hbm],
        out_specs=vmem,
        scratch_shapes=[
            pltpu.VMEM((n, rows, groups * PER * HD), BF),
            pltpu.VMEM((2, tokens, width), BF),
            pltpu.VMEM((2, tokens, width), BF),
            pltpu.VMEM((2, tokens // tb, m_rows, tb), F32),
            pltpu.VMEM((2, m_rows, HD), F32),
            pltpu.VMEM((m_rows, 2 * HD), F32),
            pltpu.VMEM((groups, chunks, m_rows, 2 * HD), F32),
            pltpu.VMEM((groups, chunks, m_rows, HD), F32),
            pltpu.VMEM((groups, PER, 3 * slots, 3 * HD), BF),
            pltpu.VMEM((all_rows, slots), BF),
            pltpu.VMEM((groups, n, part, HD), BF),
            pltpu.VMEM((groups, n, 8, part), F32),
            pltpu.VMEM((groups, n, part, HD), BF),
            pltpu.VMEM((groups, n, 8, part), F32),
            dma((4,)), dma, dma((groups, n)), dma((groups, n)),
            dma((groups, n)), dma((groups, n)), dma((groups, n)), dma((groups, n)),
        ],
        compiler_params=pltpu.CompilerParams(
            collective_id=0, has_side_effects=True, vmem_limit_bytes=60 * 1024 * 1024
        ),
        name="cascade",
    )(queries, row_branch.reshape(1, all_rows), branch_lengths, root_keys, root_values, branch_keys, branch_values)


def solution(mesh):
    placed = (
        P(("groups", "branch"), "head"),
        P(("groups", "branch"), "head"),
        P(("groups", "branch"), "head"),
        P(("groups", "branch"), None, "head"),
        P(("groups", "branch"), None, "head"),
        P(("groups", "branch")),
        P("groups"),
    )
    return jax.shard_map(
        on_device,
        mesh=mesh,
        in_specs=placed,
        out_specs=P(("groups", "branch"), "head"),
        check_vma=False,
    )
```

```python
import functools
import math

import jax
import jax.numpy as jnp
from jax import lax
from jax.experimental import pallas as pl
from jax.experimental.pallas import tpu as pltpu
from jax.sharding import PartitionSpec as P

HD = 128
PER = 8
NEG = -1e30
MESH = pl.DeviceIdType.MESH
BF = jnp.bfloat16
F32 = jnp.float32


def split(value, parts):
    pieces = []
    for _ in range(parts):
        piece = value.astype(BF)
        pieces.append(piece)
        value = value - piece.astype(F32)
    return pieces


def kernel(
    n, rows, tokens, groups, tb,
    q_ref, rb_ref, len_ref, rk_ref, rv_ref, bk_ref, bv_ref, out_ref,
    qall, kbuf, vbuf, sbuf, mbuf, acc, rnum, rm, right, spread_e,
    send_o, send_l, recv_o, recv_l,
    kv_sem, q_own, q_send, q_recv, o_send, o_recv, l_send, l_recv,
):
    me = lax.axis_index("branch")
    slots = 2 * rows
    m_rows = slots * PER
    chunks = n // 2
    all_rows = n * rows
    part = rows * PER
    blocks = tokens // tb
    factor = math.log2(math.e) / math.sqrt(HD)

    copies = [
        pltpu.make_async_copy(src, dst, kv_sem.at[i])
        for i, (src, dst) in enumerate((
            (rk_ref, kbuf.at[0]), (rv_ref, vbuf.at[0]),
            (bk_ref.at[0], kbuf.at[1]), (bv_ref.at[0], vbuf.at[1]),
        ))
    ]
    own = pltpu.make_async_copy(q_ref, qall.at[me], q_own)
    own.start()
    copies[2].start()

    barrier = pltpu.get_barrier_semaphore()
    for off in range(1, n):
        peer = me ^ off
        pl.semaphore_signal(barrier, inc=1, device_id={"branch": peer}, device_id_type=MESH)
    pl.semaphore_wait(barrier, n - 1)

    q_copies = {}
    for g in range(groups):
        for off in reversed(range(1, n)):
            peer = me ^ off
            cols = pl.ds(g * PER * HD, PER * HD)
            copy = pltpu.make_async_remote_copy(
                src_ref=q_ref.at[:, cols], dst_ref=qall.at[me, :, cols],
                send_sem=q_send.at[g, off], recv_sem=q_recv.at[g, off],
                device_id={"branch": peer}, device_id_type=MESH,
            )
            copy.start()
            q_copies[g, off] = copy
    copies[3].start()

    rb = rb_ref[...]
    mem_row = jnp.where(rb == me, 1.0, 0.0).astype(F32)
    r_sub = lax.broadcasted_iota(jnp.int32, (all_rows, all_rows), 0)
    r_lane = lax.broadcasted_iota(jnp.int32, (all_rows, all_rows), 1)
    mem_b = jnp.broadcast_to(mem_row, (all_rows, all_rows))
    mem_col = jnp.sum(jnp.where(r_sub == r_lane, mem_b, 0.0), axis=1, keepdims=True)
    rank_col = jnp.sum(jnp.where(r_lane < r_sub, mem_b, 0.0), axis=1, keepdims=True)
    mem_cb = jnp.broadcast_to(mem_col, (all_rows, all_rows))
    rank_row = jnp.sum(jnp.where(r_sub < r_lane, mem_cb, 0.0), axis=0, keepdims=True)
    slot_sub = lax.broadcasted_iota(jnp.int32, (slots, all_rows), 0).astype(F32)
    picker = jnp.where(
        (jnp.broadcast_to(rank_row, (slots, all_rows)) == slot_sub)
        & (jnp.broadcast_to(mem_row, (slots, all_rows)) > 0.5), 1.0, 0.0,
    ).astype(BF)
    slot_lane = lax.broadcasted_iota(jnp.int32, (all_rows, slots), 1).astype(F32)
    e_full = jnp.where(
        (jnp.broadcast_to(rank_col, (all_rows, slots)) == slot_lane)
        & (jnp.broadcast_to(mem_col, (all_rows, slots)) > 0.5), 1.0, 0.0,
    ).astype(BF)
    spread_e[...] = e_full
    length = len_ref[0]

    def stack(q):
        return jnp.concatenate([q[:, p * HD:(p + 1) * HD] for p in range(PER)], axis=0)

    tasks = []
    for g in range(groups):
        tasks += [(1, g, 0)] + [(0, g, k) for k in range(1, chunks)]
    tasks += [(0, g, 0) for g in range(groups)]

    waited = set()
    started = {2, 3}

    def need(index):
        if index not in waited:
            waited.add(index)
            copies[index].wait()

    def launch(index):
        if index not in started:
            started.add(index)
            copies[index].start()

    def need_q(g, off):
        key = ("q", g, off)
        if key not in waited:
            waited.add(key)
            if off > 0:
                q_copies[g, off].wait_recv()
            elif ("own",) not in waited:
                waited.add(("own",))
                own.wait()

    def stage(first, second, slot):
        if first is not None:
            src, g, k = first
            cols = slice(g * PER * HD, (g + 1) * PER * HD)
            launch(2 * src)
            need(2 * src)
            launch(2 * src + 1)
            launch(0)
            if second is not None:
                launch(1)
            if src == 0:
                need_q(g, 2 * k)
                need_q(g, 2 * k + 1)
                base = (me // 2) ^ k
                query = stack(qall[pl.ds(base * 2, 2), :, cols].reshape(slots, PER * HD))
            else:
                for off in range(n):
                    need_q(g, off)
                whole = qall[:, :, cols].reshape(all_rows, PER * HD)
                query = stack(jnp.dot(picker, whole, preferred_element_type=F32).astype(BF))
            mbuf[slot] = jnp.full((m_rows, HD), NEG, F32)
        if second is not None:
            src2, g2, k2 = second
            need(2 * src2 + 1)
            other = 1 - slot
            peak = jnp.max(mbuf[other], axis=1, keepdims=True) * factor
            mbuf[other] = jnp.broadcast_to(peak, (m_rows, HD))
            acc[...] = jnp.zeros_like(acc)

        def body(j, carry):
            start = pl.multiple_of(j * tb, tb)
            if first is not None:
                keys = kbuf[src, pl.ds(start, tb), g * HD:(g + 1) * HD]
                score = lax.dot_general(
                    query, keys, (((1,), (1,)), ((), ())), preferred_element_type=F32
                )
                if src == 1:
                    place = start + lax.broadcasted_iota(jnp.int32, (m_rows, tb), 1)
                    score = jnp.where(place < length, score, NEG)
                top = score[:, :HD]
                for i in range(1, tb // HD):
                    top = jnp.maximum(top, score[:, i * HD:(i + 1) * HD])
                sbuf[slot, j] = score
                mbuf[slot] = jnp.maximum(mbuf[slot], top)
            if second is not None:
                top2 = mbuf[other]
                peaks = jnp.concatenate([top2] * (tb // HD), axis=1)
                weights = jnp.exp2(sbuf[other, j] * factor - peaks).astype(BF)
                values = vbuf[src2, pl.ds(start, tb), g2 * HD:(g2 + 1) * HD]
                wide = jnp.concatenate([values, jnp.ones((tb, HD), BF)], axis=1)
                acc[...] += jnp.dot(weights, wide, preferred_element_type=F32)
            return carry

        lax.fori_loop(0, blocks, body, 0)

        if second is not None and src2 == 0:
            rnum[g2, k2] = acc[...]
            rm[g2, k2] = mbuf[other]
        elif second is not None:
            numer, total, top = acc[:, :HD], acc[:, HD:], mbuf[other]
            for p in range(PER):
                lo, hi = p * slots, (p + 1) * slots
                gap = [jnp.zeros((slots, HD), BF)]
                pieces = (split(numer[lo:hi], 2) + gap, split(total[lo:hi], 2) + gap, split(top[lo:hi], 3))
                right[g2, p] = jnp.concatenate(
                    [jnp.concatenate(piece, axis=0) for piece in pieces], axis=1
                )

    eye = (
        lax.broadcasted_iota(jnp.int32, (part, part), 0)
        == lax.broadcasted_iota(jnp.int32, (part, part), 1)
    )
    sent = []

    def finish(g, k):
        base = (me // 2) ^ k
        e = spread_e[pl.ds(pl.multiple_of(base * slots, slots), slots), :]
        e3 = jnp.concatenate([e, e, e], axis=1)
        has = jnp.sum(e.astype(F32), axis=1, keepdims=True) > 0.5
        has = jnp.broadcast_to(has, (slots, HD))
        whole_o, whole_l = [], []
        for p in range(PER):
            lo, hi = p * slots, (p + 1) * slots
            back = jnp.dot(e3, right[g, p], preferred_element_type=F32)
            r_num = rnum[g, k, lo:hi, :HD]
            r_tot = rnum[g, k, lo:hi, HD:]
            r_top = rm[g, k, lo:hi]
            b_top = jnp.where(has, back[:, 2 * HD:], NEG)
            peak = jnp.maximum(r_top, b_top)
            x = jnp.exp2(r_top - peak)
            y = jnp.exp2(b_top - peak)
            num = r_num * x + back[:, :HD] * y
            tot = r_tot * x + back[:, HD:2 * HD] * y
            whole_o.append((num / tot).astype(BF))
            whole_l.append(peak + jnp.log2(tot))
        for half in range(2):
            off_slot = 2 * k + half
            lo, hi = half * rows, (half + 1) * rows
            send_o[g, off_slot] = jnp.concatenate([o[lo:hi] for o in whole_o], axis=0)
            lse = jnp.concatenate([v[lo:hi] for v in whole_l], axis=0)
            line = jnp.sum(jnp.where(eye, lse, 0.0), axis=0, keepdims=True)
            send_l[g, off_slot] = jnp.broadcast_to(line, (8, part))
        for off in range(max(1, 2 * k), 2 * k + 2):
            peer = me ^ off
            index = 2 * k + lax.rem(peer, 2)
            pair = []
            for src, dst, s_sem, r_sem in (
                (send_o, recv_o, o_send, o_recv), (send_l, recv_l, l_send, l_recv),
            ):
                copy = pltpu.make_async_remote_copy(
                    src_ref=src.at[g, index], dst_ref=dst.at[g, off],
                    send_sem=s_sem.at[g, off], recv_sem=r_sem.at[g, off],
                    device_id={"branch": peer}, device_id_type=MESH,
                )
                copy.start()
                pair.append(copy)
            sent.append((g, off, pair))

    def collect(g):
        mine = lax.rem(me, 2)
        lines = [send_l[g, mine][:1]]
        outs = [send_o[g, mine]]
        for gg, off, pair in sent:
            if gg == g:
                for copy in pair:
                    copy.wait_recv()
                lines.append(recv_l[g, off][:1])
                outs.append(recv_o[g, off])
        peak = functools.reduce(jnp.maximum, lines)
        scales = [jnp.exp2(line - peak) for line in lines]
        inverse = 1.0 / functools.reduce(jnp.add, scales)
        result = jnp.zeros((part, HD), F32)
        for scale, o in zip(scales, outs):
            diag = jnp.where(eye, jnp.broadcast_to(scale * inverse, (part, part)), 0.0)
            left = jnp.concatenate(split(diag, 2), axis=1)
            result += jnp.dot(left, jnp.concatenate([o, o], axis=0), preferred_element_type=F32)
        result = result.astype(BF)
        for p in range(PER):
            out_ref[:, (g * PER + p) * HD:(g * PER + p + 1) * HD] = result[p * rows:(p + 1) * rows]

    previous = None
    done, finished = set(), set()
    for t, task in enumerate(tasks + [None]):
        stage(task, previous, t % 2)
        if previous is not None:
            done.add(previous)
            for g in range(groups):
                for k in reversed(range(chunks)):
                    if (1, g, 0) in done and (0, g, k) in done and (g, k) not in finished:
                        finished.add((g, k))
                        finish(g, k)
        previous = task
    for g in range(groups):
        collect(g)
    for copy in q_copies.values():
        copy.wait_send()
    for _, _, pair in sent:
        for copy in pair:
            copy.wait_send()


def on_device(
    queries, root_keys, root_values, branch_keys, branch_values, branch_lengths, row_branch
):
    rows = queries.shape[0]
    all_rows = row_branch.shape[0]
    n = all_rows // rows
    tokens, width = root_keys.shape
    groups = width // HD
    chunks = n // 2
    slots = 2 * rows
    m_rows = slots * PER
    part = rows * PER
    tb = min(2048, tokens)
    vmem = pl.BlockSpec(memory_space=pltpu.VMEM)
    smem = pl.BlockSpec(memory_space=pltpu.SMEM)
    hbm = pl.BlockSpec(memory_space=pl.ANY)
    dma = pltpu.SemaphoreType.DMA
    return pl.pallas_call(
        functools.partial(kernel, n, rows, tokens, groups, tb),
        out_shape=jax.ShapeDtypeStruct(queries.shape, BF),
        in_specs=[vmem, vmem, smem, hbm, hbm, hbm, hbm],
        out_specs=vmem,
        scratch_shapes=[
            pltpu.VMEM((n, rows, groups * PER * HD), BF),
            pltpu.VMEM((2, tokens, width), BF),
            pltpu.VMEM((2, tokens, width), BF),
            pltpu.VMEM((2, tokens // tb, m_rows, tb), F32),
            pltpu.VMEM((2, m_rows, HD), F32),
            pltpu.VMEM((m_rows, 2 * HD), F32),
            pltpu.VMEM((groups, chunks, m_rows, 2 * HD), F32),
            pltpu.VMEM((groups, chunks, m_rows, HD), F32),
            pltpu.VMEM((groups, PER, 3 * slots, 3 * HD), BF),
            pltpu.VMEM((all_rows, slots), BF),
            pltpu.VMEM((groups, n, part, HD), BF),
            pltpu.VMEM((groups, n, 8, part), F32),
            pltpu.VMEM((groups, n, part, HD), BF),
            pltpu.VMEM((groups, n, 8, part), F32),
            dma((4,)), dma, dma((groups, n)), dma((groups, n)),
            dma((groups, n)), dma((groups, n)), dma((groups, n)), dma((groups, n)),
        ],
        compiler_params=pltpu.CompilerParams(
            collective_id=0, has_side_effects=True, vmem_limit_bytes=60 * 1024 * 1024
        ),
        name="cascade",
    )(queries, row_branch.reshape(1, all_rows), branch_lengths, root_keys, root_values, branch_keys, branch_values)


def solution(mesh):
    placed = (
        P(("groups", "branch"), "head"),
        P(("groups", "branch"), "head"),
        P(("groups", "branch"), "head"),
        P(("groups", "branch"), None, "head"),
        P(("groups", "branch"), None, "head"),
        P(("groups", "branch")),
        P("groups"),
    )
    return jax.shard_map(
        on_device,
        mesh=mesh,
        in_specs=placed,
        out_specs=P(("groups", "branch"), "head"),
        check_vma=False,
    )
```
